512 devices in a mesh: gz: 128 (over z, y, core), row: 4 (over x).
Axes of the slice: x: 4, y: 4, z: 16, core: 2. Of those that a mesh axis runs over, the one named last changes fastest.
Arguments:
- tokens: bfloat16 [262144, 384], P(('gz', 'row')), may hold values from -6 to 6
- key_blocks: int32 [4096, 20], P(('gz', 'row')), may hold values from 0 to 4095, as said below
- counts: int32 [128], replicated, may hold values from 8 to 32, as said below
- norm_gain: float32 [384], replicated, may hold values from 0.1 to 1.9
- qkv_weight: bfloat16 [384, 1152], replicated, may hold values from -1 to 1
- out_weight: bfloat16 [384, 384], replicated, may hold values from -0.3125 to 0.3125
- mlp_gain: float32 [384], replicated, may hold values from 0.1 to 1.9
- up_weight: bfloat16 [384, 1536], replicated, may hold values from -0.3125 to 0.3125
- down_weight: bfloat16 [1536, 384], replicated, may hold values from -0.15625 to 0.15625
Outputs:
- block_out: bfloat16 [262144, 384], P(('gz', 'row'))
The draws below stay inside these ranges and needn't reach their ends.
Inputs may be any that keep to these rules, and one draw needn't show every extreme that they name: `key_blocks`: entries 0 to 3 of a query block's list name live blocks of the query's own slab (repeats possible). The other 16 entries name blocks with the same row group as the query block (id % 32 // 8 equal), in any slab; over the blocks of one device each slab is named by exactly 1 such entries. `counts`: one slab is full in every draw.
All inputs are finite; a program needn't handle non-finite values.
Results may differ from the reference program's by a relative error of at most 0.01.
Values may be sent and summed in bfloat16 or wider, within the bound.
A program may use at most 128 MiB of HBM per device.

```python
import jax
import jax.numpy as jnp
from jax import lax

D = 384
H = 12
FF = 1536
QB_DEV = 8
NNEAR = 4
NFAR = 16
NSEL = 20
QB_SLAB = 32
NB = 4096
TOKENS = 262144


def shared_layout(key):
    base = jax.random.fold_in(key, 31)
    slabs_all = NB // QB_SLAB
    devices_all = NB // QB_DEV
    rows_slab = QB_SLAB // QB_DEV
    count_key, fill_key, near_key, far_key, local_key = jax.random.split(base, 5)
    slab_counts = jax.random.randint(count_key, (slabs_all,), QB_SLAB // 4, QB_SLAB + 1)
    full_slab = jax.random.randint(fill_key, (), 0, slabs_all)
    slab_counts = jnp.where(jnp.arange(slabs_all) == full_slab, QB_SLAB, slab_counts).astype(jnp.int32)
    device_ids = jnp.arange(devices_all)
    device_slab = device_ids // rows_slab
    device_row = device_ids % rows_slab
    near_pick = jax.random.randint(near_key, (devices_all, QB_DEV, NNEAR), 0, 1 << 20)
    near_within = near_pick % slab_counts[device_slab][:, None, None]
    near_ids = device_slab[:, None, None] * QB_SLAB + near_within
    base_list = jnp.repeat(jnp.arange(slabs_all), QB_DEV * NFAR // slabs_all)
    perm_keys = jax.random.split(far_key, devices_all)
    far_slabs = jax.vmap(lambda one_key: jax.random.permutation(one_key, base_list))(perm_keys)
    far_local = jax.random.randint(local_key, (devices_all, QB_DEV * NFAR), 0, QB_DEV)
    first_device = (device_ids == 0)[:, None] & (far_slabs == 0)
    last_device = (device_ids == devices_all - 1)[:, None] & (far_slabs == slabs_all - 1)
    far_local = jnp.where(first_device, 0, far_local)
    far_local = jnp.where(last_device, QB_DEV - 1, far_local)
    far_ids = far_slabs * QB_SLAB + device_row[:, None] * QB_DEV + far_local
    far_ids = far_ids.reshape(devices_all, QB_DEV, NFAR)
    block_ids = jnp.concatenate([near_ids, far_ids], axis=2).reshape(NB, NSEL)
    return (block_ids.astype(jnp.int32), slab_counts)


def draw_key_blocks(key, part):
    return shared_layout(key)[0]


def draw_counts(key, part):
    return shared_layout(key)[1]


def draw_tokens(key, part):
    base = jax.random.fold_in(key, 7)
    noise_key = jax.random.fold_in(base, 0)
    drawn = jax.random.normal(noise_key, (TOKENS, D), jnp.float32)
    return jnp.clip(drawn, -6.0, 6.0).astype(jnp.bfloat16)


def draw_qkv_weight(key, part):
    base = jax.random.fold_in(key, 11)
    scale = float(D) ** (-0.5)
    columns = jnp.arange(3 * D)
    column_scale = jnp.where(columns < 2 * D, 2.0, 1.0).astype(jnp.float32)
    values = jnp.clip(jax.random.normal(base, (D, 3 * D), jnp.float32), -6.0, 6.0) * scale * column_scale[None, :]
    return jnp.clip(values, -1.0, 1.0).astype(jnp.bfloat16)


def gaussian(key, extent, scale, reach, dtype=jnp.bfloat16):
    return jnp.clip(scale * jax.random.normal(key, extent, jnp.float32), -reach, reach).astype(dtype)


def setup_inputs(seed: int = 0) -> dict:
    splits = jax.random.split(jax.random.key(seed), 10)
    return {
        "tokens": draw_tokens(jax.random.fold_in(splits[9], 71), 0),
        "key_blocks": draw_key_blocks(jax.random.fold_in(splits[9], 71), 0),
        "counts": draw_counts(jax.random.fold_in(splits[9], 71), 0),
        "norm_gain": jnp.clip(1.0 + 0.18 * jax.random.normal(splits[3], (D,), jnp.float32), 0.1, 1.9),
        "qkv_weight": draw_qkv_weight(jax.random.fold_in(splits[9], 71), 0),
        "out_weight": gaussian(splits[5], (D, D), D ** -0.5, 0.3125),
        "mlp_gain": jnp.clip(1.0 + 0.18 * jax.random.normal(splits[6], (D,), jnp.float32), 0.1, 1.9),
        "up_weight": gaussian(splits[7], (D, FF), D ** -0.5, 0.3125),
        "down_weight": gaussian(splits[8], (FF, D), FF ** -0.5, 0.15625),
    }


def rms_norm(values, gain):
    mean_sq = lax.optimization_barrier(jnp.mean(values * values, axis=-1, keepdims=True))
    return values * lax.rsqrt(mean_sq + 1e-05) * gain

def attend(query_block, key_values, live_blocks):
    model_width = query_block.shape[1]
    head_size = model_width // H
    keys = key_values[:, :, :model_width].reshape(-1, H, head_size).astype(jnp.float32)
    values = key_values[:, :, model_width:].reshape(-1, H, head_size).astype(jnp.float32)
    heads = query_block.reshape(-1, H, head_size).astype(jnp.float32)
    scores = jnp.einsum('qhd,khd->hqk', heads, keys) / jnp.sqrt(jnp.float32(head_size))
    key_live = jnp.repeat(live_blocks, key_values.shape[1])
    scores = jnp.where(key_live[None, None, :], scores, jnp.float32(-1e+30))
    top = lax.optimization_barrier(jnp.max(scores, axis=-1, keepdims=True))
    weights = jnp.exp(scores - top)
    total = lax.optimization_barrier(jnp.sum(weights, axis=-1))
    rounded = weights.astype(jnp.bfloat16).astype(jnp.float32)
    mixed = jnp.einsum('hqk,khd->qhd', rounded, values) / jnp.transpose(total)[:, :, None]
    return mixed.reshape(-1, model_width).astype(jnp.bfloat16)

def reference(tokens, key_blocks, counts, norm_gain, qkv_weight, out_weight, mlp_gain, up_weight, down_weight):
    model_width = tokens.shape[1]
    block_count = key_blocks.shape[0]
    block_len = tokens.shape[0] // block_count
    inputs = tokens.astype(jnp.float32)
    normed = rms_norm(inputs, norm_gain).astype(jnp.bfloat16)
    projected = jnp.dot(normed, qkv_weight, preferred_element_type=jnp.float32).astype(jnp.bfloat16)
    queries = projected[:, :model_width].reshape(block_count, block_len, model_width)
    key_values = projected[:, model_width:].reshape(block_count, block_len, 2 * model_width)
    owner_slab = key_blocks // QB_SLAB
    within = key_blocks % QB_SLAB
    live = within < counts[owner_slab]

    def one_block(packed):
        query_block, block_ids, live_blocks = packed
        return attend(query_block, key_values[block_ids], live_blocks)
    attended = lax.map(one_block, (queries, key_blocks, live)).reshape(-1, model_width)
    residual = (inputs + jnp.dot(attended, out_weight, preferred_element_type=jnp.float32)).astype(jnp.bfloat16)
    normed_two = rms_norm(residual.astype(jnp.float32), mlp_gain).astype(jnp.bfloat16)
    hidden = jax.nn.gelu(jnp.dot(normed_two, up_weight, preferred_element_type=jnp.float32)).astype(jnp.bfloat16)
    result = residual.astype(jnp.float32) + jnp.dot(hidden, down_weight, preferred_element_type=jnp.float32)
    return result.astype(jnp.bfloat16)
```

```python
import functools

import jax
import jax.numpy as jnp
from jax import lax
from jax.experimental import pallas as pl
from jax.experimental.pallas import tpu as pltpu
from jax.sharding import PartitionSpec as P

H = 12
NNEAR = 4
NFAR = 16
NZ = 16
NJ = 8
NX = 4
MESH = pl.DeviceIdType.MESH


def rms_norm(values, gain):
    mean_sq = jnp.mean(values * values, axis=-1, keepdims=True)
    return values * lax.rsqrt(mean_sq + 1e-05) * gain


def comm_kernel(tok_ref, gain_ref, req_ref, far_ref, near_ref, nrm_ref, *scratch):
    fwd = scratch[0:7]
    bwd = scratch[7:14]
    opp = scratch[14]
    send_buf, req_in, req_s = scratch[15:18]
    fs_sem, fr_sem, bs_sem, br_sem, ys_sem, yr_sem, xs_sem, xr_sem, qs_sem, qr_sem, loc_sem = scratch[18:]
    gz = lax.axis_index("gz")
    x = lax.axis_index("row")
    z = gz // NJ
    j = lax.rem(gz, NJ)
    z_up = lax.rem(z + 1, NZ) * NJ + j
    z_down = lax.rem(z + NZ - 1, NZ) * NJ + j

    def plane(o):
        return z * NJ + lax.rem(j + o, NJ)

    def along(o):
        return lax.rem(x + o, NX)

    barrier = pltpu.get_barrier_semaphore()
    for peer in (z_up, z_down):
        pl.semaphore_signal(barrier, inc=1, device_id=(peer, x), device_id_type=MESH)
    for o in range(1, NJ):
        pl.semaphore_signal(barrier, inc=1, device_id=(plane(o), x), device_id_type=MESH)
    for o in range(1, NX):
        pl.semaphore_signal(barrier, inc=1, device_id=(gz, along(o)), device_id_type=MESH)
    pl.semaphore_wait(barrier, 2 + NJ - 1 + NX - 1)

    def req_copy(o):
        return pltpu.make_async_remote_copy(
            src_ref=req_ref.at[NJ - o], dst_ref=req_in.at[o],
            send_sem=qs_sem.at[o], recv_sem=qr_sem.at[o],
            device_id=(plane(NJ - o), x), device_id_type=MESH)

    for o in range(1, NJ):
        req_copy(o).start()
    req_in[0] = req_ref[0]

    values = tok_ref[...].astype(jnp.float32)
    nrm_ref[...] = rms_norm(values, gain_ref[...]).astype(jnp.bfloat16)

    half = NJ // 2

    def ring(k, h, forward):
        slots = fwd if forward else bwd
        src = nrm_ref if k == 1 else slots[k - 2]
        dst = opp if k == 8 else slots[k - 1]
        part = pl.ds(h * half, half)
        return pltpu.make_async_remote_copy(
            src_ref=src.at[part], dst_ref=dst.at[part],
            send_sem=(fs_sem if forward else bs_sem).at[k, h],
            recv_sem=(fr_sem if forward else br_sem).at[k, h],
            device_id=(z_up if forward else z_down, x), device_id_type=MESH)

    def near_copy(o):
        return pltpu.make_async_remote_copy(
            src_ref=nrm_ref, dst_ref=near_ref.at[o],
            send_sem=xs_sem.at[o], recv_sem=xr_sem.at[o],
            device_id=(gz, along(o)), device_id_type=MESH)

    for h in range(2):
        ring(1, h, True).start()
        ring(1, h, False).start()
    for o in range(1, NX):
        near_copy(o).start()
    near_ref[0] = nrm_ref[...]
    for o in range(1, NJ):
        req_copy(o).wait_recv()
    copy = pltpu.make_async_copy(req_in, req_s, loc_sem)
    copy.start()
    copy.wait()

    def plane_copy(k, o):
        first, count = (0, 1) if k == 0 else (15, 1) if k == 8 else (2 * k - 1, 2)
        part = pl.ds(first, count)
        return pltpu.make_async_remote_copy(
            src_ref=send_buf.at[o, part], dst_ref=far_ref.at[o, part],
            send_sem=ys_sem.at[k, o], recv_sem=yr_sem.at[k, o],
            device_id=(plane(o), x), device_id_type=MESH)

    def forward_plane(k, held):
        for p, ref in held:
            far_ref[0, p] = ref[req_s[0, 0, p]]

        def one(o, carry):
            for p, ref in held:
                send_buf[o, p] = ref[req_s[o, 0, p]]
            plane_copy(k, o).start()
            return carry

        lax.fori_loop(1, NJ, one, 0)

    forward_plane(0, [(0, nrm_ref)])
    for k in range(1, 8):
        for h in range(2):
            ring(k, h, True).wait_recv()
            if k < 7 or h == 0:
                ring(k + 1, h, True).start()
            ring(k, h, False).wait_recv()
            if k < 7 or h == 1:
                ring(k + 1, h, False).start()
        forward_plane(k, [(2 * k - 1, bwd[k - 1]), (2 * k, fwd[k - 1])])
    ring(8, 0, True).wait_recv()
    ring(8, 1, False).wait_recv()
    forward_plane(8, [(15, opp)])

    for o in range(1, NX):
        near_copy(o).wait_recv()
    for k in range(9):
        def arrive(o, carry, k=k):
            plane_copy(k, o).wait_recv()
            return carry
        lax.fori_loop(1, NJ, arrive, 0)
    for k in range(1, 9):
        for h in range(2):
            if k < 8 or h == 0:
                ring(k, h, True).wait_send()
            if k < 8 or h == 1:
                ring(k, h, False).wait_send()
    for o in range(1, NX):
        near_copy(o).wait_send()
    for o in range(1, NJ):
        req_copy(o).wait_send()
    for k in range(9):
        def left(o, carry, k=k):
            plane_copy(k, o).wait_send()
            return carry
        lax.fori_loop(1, NJ, left, 0)


def exchange(tokens, gain, requests):
    blocks, length, width = tokens.shape
    vmem = pl.BlockSpec(memory_space=pltpu.VMEM)
    block = (blocks, length, width)
    bf16 = jnp.bfloat16
    dma = pltpu.SemaphoreType.DMA
    return pl.pallas_call(
        comm_kernel,
        name="exchange",
        out_shape=(
            jax.ShapeDtypeStruct((NJ, NZ, length, width), bf16),
            jax.ShapeDtypeStruct((NX, blocks, length, width), bf16),
            jax.ShapeDtypeStruct(block, bf16),
        ),
        in_specs=[vmem] * 3,
        out_specs=(vmem,) * 3,
        scratch_shapes=[pltpu.VMEM(block, bf16)] * 15
        + [
            pltpu.VMEM((NJ, NZ, length, width), bf16),
            pltpu.VMEM((NJ, 1, 128), jnp.int32),
            pltpu.SMEM((NJ, 1, 128), jnp.int32),
            dma((9, 2)), dma((9, 2)), dma((9, 2)), dma((9, 2)),
            dma((9, NJ)), dma((9, NJ)),
            dma((NX,)), dma((NX,)),
            dma((NJ,)), dma((NJ,)),
            dma,
        ],
        compiler_params=pltpu.CompilerParams(
            collective_id=0, has_side_effects=True, vmem_limit_bytes=60 << 20
        ),
    )(tokens, gain, requests)


def block_kernel(
    pos_ref, live_ref, tok_ref, nrm_ref, far_ref, near_ref, wq_ref, wk_ref, wv_ref, wo_ref,
    gain_ref, up_ref, down_ref, out_ref, qp_ref, stage_ref, mixed_ref, att_ref
):
    tokens, width = tok_ref.shape
    own = tokens // 64
    f32, bf16 = jnp.float32, jnp.bfloat16
    head = width // H
    scale = 1.4426950408889634 / (head ** 0.5)
    wide = qp_ref.shape[2]
    lane = lax.broadcasted_iota(jnp.int32, (64, wide - width), 1)

    queries = jnp.dot(nrm_ref[...], wq_ref[...], preferred_element_type=f32).astype(bf16)
    group = lax.broadcasted_iota(jnp.int32, (tokens, 128), 1) // head
    for h in range(H):
        g = h * head // 128
        cols = slice(g * 128, g * 128 + 128)
        part = jnp.where(group == h % (128 // head), queries[:, cols], jnp.zeros((), bf16))
        folded = lax.dot_general(
            part, wk_ref[:, cols], (((1,), (1,)), ((), ())), preferred_element_type=f32
        )
        folded = (folded * scale).astype(bf16)
        for b in range(own):
            qp_ref[b, h * 64:(h + 1) * 64, :width] = folded[b * 64:(b + 1) * 64]
            qp_ref[b, h * 64:(h + 1) * 64, width:] = jnp.where(lane == 1, 1.0, 0.0).astype(bf16)

    def one_block(b, carry):
        for n in range(NNEAR + NFAR):
            rows = slice(n * 64, n * 64 + 64)
            ref = near_ref if n < NNEAR else far_ref
            stage_ref[rows, :width] = ref[pos_ref[b, n]]
            bias = jnp.where(live_ref[b, n] > 0, 0.0, -1e30)
            stage_ref[rows, width:] = jnp.where(
                lane == 0, 1.0, jnp.where(lane == 1, bias, 0.0)).astype(bf16)
        rows_c = 256
        for c in range(H * 64 // rows_c):
            rows = slice(c * rows_c, (c + 1) * rows_c)
            scores = lax.dot_general(
                qp_ref[b, rows], stage_ref[...], (((1,), (1,)), ((), ())), preferred_element_type=f32
            )
            top = jnp.max(scores, axis=-1, keepdims=True)
            weights = jnp.exp2(scores - top).astype(bf16)
            mixed = jnp.dot(weights, stage_ref[...], preferred_element_type=f32)
            total = mixed[:, width:width + 1]
            result = (mixed[:, :width] / total).astype(bf16)
            for i in range(rows_c // 64):
                mixed_ref[c * (rows_c // 64) + i, pl.ds(b * 64, 64)] = result[i * 64:(i + 1) * 64]
        return carry

    lax.fori_loop(0, own, one_block, 0)

    wgroup = lax.broadcasted_iota(jnp.int32, (width, 128), 1) // head
    for g in range(width // 128):
        cols = slice(g * 128, g * 128 + 128)
        acc = jnp.zeros((tokens, 128), f32)
        for i in range(128 // head):
            part = jnp.where(wgroup == i, wv_ref[:, cols], jnp.zeros((), bf16))
            acc += jnp.dot(mixed_ref[g * (128 // head) + i], part, preferred_element_type=f32)
        att_ref[:, cols] = acc.astype(bf16)

    residual = (
        tok_ref[...].astype(f32) + jnp.dot(att_ref[...], wo_ref[...], preferred_element_type=f32)
    ).astype(bf16)
    residual = residual.astype(f32)
    second = rms_norm(residual, gain_ref[...]).astype(bf16)
    hidden = jax.nn.gelu(jnp.dot(second, up_ref[...], preferred_element_type=f32)).astype(bf16)
    result = residual + jnp.dot(hidden, down_ref[...], preferred_element_type=f32)
    out_ref[...] = result.astype(bf16)


def attention(pos, live, tokens, normed, far, near, wq, wk, wv, wo, gain, up, down):
    count, width = tokens.shape
    vmem = pl.BlockSpec(memory_space=pltpu.VMEM)
    smem = pl.BlockSpec(memory_space=pltpu.SMEM)
    bf16 = jnp.bfloat16
    return pl.pallas_call(
        block_kernel,
        name="attention",
        out_shape=jax.ShapeDtypeStruct(tokens.shape, bf16),
        in_specs=[smem] * 2 + [vmem] * 11,
        out_specs=vmem,
        scratch_shapes=[
            pltpu.VMEM((count // 64, H * 64, 512), bf16),
            pltpu.VMEM(((NNEAR + NFAR) * 64, 512), bf16),
            pltpu.VMEM((H, count, width), bf16),
            pltpu.VMEM((count, width), bf16),
        ],
        compiler_params=pltpu.CompilerParams(vmem_limit_bytes=60 << 20),
    )(pos, live, tokens, normed, far, near, wq, wk, wv, wo, gain, up, down)


def body(
    tokens, key_blocks, counts, norm_gain, qkv_weight, out_weight, mlp_gain, up_weight, down_weight
):
    width = tokens.shape[1]
    own = key_blocks.shape[0]
    length = tokens.shape[0] // own
    slabs = counts.shape[0]
    gz = lax.axis_index("gz")
    x = lax.axis_index("row")
    z, j = gz // NJ, gz % NJ
    slab_blocks = own * NX
    owner = key_blocks // slab_blocks
    within = key_blocks % slab_blocks
    table = jnp.arange(slabs, dtype=jnp.int32)
    slab_count = jnp.sum(jnp.where(owner[:, :, None] == table, counts, 0), axis=-1)
    live = (within < slab_count).astype(jnp.int32)

    place = jnp.arange(NZ, dtype=jnp.int32)
    z_off = jnp.where(place == 15, 8, jnp.where(place % 2 == 1, (place + 1) // 2, (NZ - place // 2) % NZ))
    want = ((z + z_off) % NZ)[None, :] * NJ + ((j + jnp.arange(NJ, dtype=jnp.int32)) % NJ)[:, None]
    far_owner = owner[:, NNEAR:].reshape(-1)
    far_local = (key_blocks[:, NNEAR:] % own).reshape(-1)
    requests = jnp.sum(
        jnp.where(want[:, :, None] == far_owner, far_local, 0), axis=-1)
    requests = jnp.pad(requests, ((0, 0), (0, 128 - NZ))).reshape(NJ, 1, 128)

    z_rel = (owner // NJ - z) % NZ
    order = jnp.where(z_rel == 0, 0, jnp.where(z_rel == 8, 15, jnp.where(z_rel < 8, 2 * z_rel - 1, 2 * (NZ - z_rel))))
    far_pos = ((j - owner % NJ) % NJ) * NZ + order
    near_pos = ((x - within // own) % NX) * own + within % own
    column = jnp.arange(key_blocks.shape[1])[None, :]
    pos = jnp.where(column < NNEAR, near_pos, far_pos)

    far, near, normed = exchange(
        tokens.reshape(own, length, width), norm_gain.reshape(1, 1, width), requests)
    return attention(
        pos, live, tokens, normed.reshape(-1, width), far.reshape(-1, length, width), near.reshape(-1, length, width),
        qkv_weight[:, :width], qkv_weight[:, width:2 * width], qkv_weight[:, 2 * width:],
        out_weight, mlp_gain.reshape(1, width), up_weight, down_weight)


def solution(mesh):
    return jax.shard_map(
        body,
        mesh=mesh,
        in_specs=(
            P(("gz", "row"), None),
            P(("gz", "row"), None),
            P(),
            P(),
            P(),
            P(),
            P(),
            P(),
            P(),
        ),
        out_specs=P(("gz", "row"), None),
        check_vma=False,
    )
```

```python
import functools

import jax
import jax.numpy as jnp
from jax import lax
from jax.experimental import pallas as pl
from jax.experimental.pallas import tpu as pltpu
from jax.sharding import PartitionSpec as P

H = 12
NNEAR = 4
NFAR = 16
NZ = 16
NJ = 8
NX = 4
BLOCK = 64
HEADS = 6
LANES = 256
SPARE = 192
ROWS = (48, 16)
PIECES = 4
MESH = pl.DeviceIdType.MESH
F32, BF16 = jnp.float32, jnp.bfloat16


def rms_norm(values, gain):
    mean_sq = jnp.mean(values * values, axis=-1, keepdims=True)
    return values * lax.rsqrt(mean_sq + 1e-05) * gain


def matmul(a, b):
    return jnp.dot(a, b, preferred_element_type=F32)


def ring_places(k):
    return (0, 1) if k == 0 else (15, 1) if k == 8 else (2 * k - 1, 2)


def fused_kernel(
    kb_ref, counts_ref, tok_ref, gain_ref, gain2_ref, qkv_any, wo_any, up_any, down_any, out_ref, *scratch
):
    scratch = list(scratch)
    passes = len(ROWS)

    def take(n):
        got = scratch[:n]
        del scratch[:n]
        return got

    own_rows = take(passes)
    slots = [take(15) for _ in range(passes)]
    send = take(passes)
    far = take(passes)
    kv_far = take(passes)
    kv_near = take(passes)
    near, normed, qkv_w, wo_w, up_w, down_w = take(6)
    wq_x, wkv_x, wo_x, q_ref, stage, s_ref, p_ref, acc_ref, top_ref, att = take(10)
    req_out, req_in, req_s = take(3)
    fs_sem, fr_sem, bs_sem, br_sem, ys_sem, yr_sem, xs_sem, xr_sem, qs_sem, qr_sem, loc_sem = take(11)

    tokens, width = tok_ref.shape
    own = tokens // BLOCK
    gz = lax.axis_index("gz")
    x = lax.axis_index("row")
    z = gz // NJ
    j = lax.rem(gz, NJ)
    z_up = lax.rem(z + 1, NZ) * NJ + j
    z_down = lax.rem(z + NZ - 1, NZ) * NJ + j

    def plane(o):
        return z * NJ + lax.rem(j + o, NJ)

    def along(o):
        return lax.rem(x + o, NX)

    barrier = pltpu.get_barrier_semaphore()
    for peer in (z_up, z_down):
        pl.semaphore_signal(barrier, inc=1, device_id=(peer, x), device_id_type=MESH)
    for o in range(1, NJ):
        pl.semaphore_signal(barrier, inc=1, device_id=(plane(o), x), device_id_type=MESH)
    for o in range(1, NX):
        pl.semaphore_signal(barrier, inc=1, device_id=(gz, along(o)), device_id_type=MESH)

    weights = [
        pltpu.make_async_copy(src, dst, loc_sem.at[i])
        for i, (src, dst) in enumerate(
            ((qkv_any, qkv_w), (wo_any, wo_w), (up_any, up_w), (down_any, down_w)))
    ]
    for copy in weights:
        copy.start()

    normed[...] = rms_norm(tok_ref[...].astype(F32), gain_ref[...]).astype(BF16)
    first = 0
    for m, rows in enumerate(ROWS):
        for b in range(own):
            own_rows[m][b] = normed[b * BLOCK + first:b * BLOCK + first + rows]
        first += rows
    for b in range(own):
        near[0, b] = normed[b * BLOCK:(b + 1) * BLOCK]

    place = lax.broadcasted_iota(jnp.int32, (NJ, 128), 1)
    offset = lax.broadcasted_iota(jnp.int32, (NJ, 128), 0)
    z_off = jnp.where(place == 15, 8, jnp.where((place & 1) == 1, (place + 1) >> 1, NZ - (place >> 1)))
    slab = ((z + z_off) & (NZ - 1)) * NJ + ((j + offset) & (NJ - 1))
    wanted = jnp.zeros((NJ, 128), jnp.int32)
    for b in range(own):
        for n in range(NNEAR, NNEAR + NFAR):
            block = kb_ref[b, n]
            wanted = jnp.where(slab == (block >> 5), block & 7, wanted)
    for r in range(NJ):
        req_out[r] = wanted[r:r + 1]
    req_in[0] = wanted[0:1]

    pl.semaphore_wait(barrier, 2 + NJ - 1 + NX - 1)

    def req_copy(o):
        return pltpu.make_async_remote_copy(
            src_ref=req_out.at[NJ - o], dst_ref=req_in.at[o],
            send_sem=qs_sem.at[o], recv_sem=qr_sem.at[o],
            device_id=(plane(NJ - o), x), device_id_type=MESH)

    def ring(m, k, h, up):
        src = own_rows[m] if k == 1 else slots[m][(0 if up else 7) + k - 2]
        dst = slots[m][14] if k == 8 else slots[m][(0 if up else 7) + k - 1]
        size = NJ // PIECES
        part = pl.ds(h * size, size)
        return pltpu.make_async_remote_copy(
            src_ref=src.at[part], dst_ref=dst.at[part],
            send_sem=(fs_sem if up else bs_sem).at[m, k, h],
            recv_sem=(fr_sem if up else br_sem).at[m, k, h],
            device_id=(z_up if up else z_down, x), device_id_type=MESH)

    def in_ring(k, h, up):
        return k < 8 or (k == 8 and (h < PIECES // 2) == up)

    def near_copy(o):
        return pltpu.make_async_remote_copy(
            src_ref=near.at[0], dst_ref=near.at[o],
            send_sem=xs_sem.at[o], recv_sem=xr_sem.at[o],
            device_id=(gz, along(o)), device_id_type=MESH)

    def plane_copy(m, k, o, count):
        at = pl.ds(*ring_places(k))
        to = pl.ds(o, count)
        return pltpu.make_async_remote_copy(
            src_ref=send[m].at[to, at], dst_ref=far[m].at[to, at],
            send_sem=ys_sem.at[m, k], recv_sem=yr_sem.at[m, k],
            device_id=(plane(o), x), device_id_type=MESH)

    def to_plane(m, k):
        at, count = ring_places(k)
        if k == 0:
            held = [(0, own_rows[m])]
        elif k == 8:
            held = [(15, slots[m][14])]
        else:
            held = [(at, slots[m][7 + k - 1]), (at + 1, slots[m][k - 1])]

        def one(o, carry):
            for p, ref in held:
                send[m][o, p] = ref[req_s[o, 0, p]]
            plane_copy(m, k, o, 1).start()
            return carry

        lax.fori_loop(1, NJ, one, 0)
        for p, ref in held:
            far[m][0, p] = ref[req_s[0, 0, p]]

    lane = lax.broadcasted_iota(jnp.int32, (1, LANES), 1)

    def prepare():
        row = lax.broadcasted_iota(jnp.int32, (width, 2 * LANES), 0)
        col = lax.broadcasted_iota(jnp.int32, (width, 2 * LANES), 1)
        inner = col & (LANES - 1)
        spread = ((inner < SPARE) & (row == (col >> 8) * SPARE + inner)).astype(F32).astype(BF16)
        weights[0].wait()
        wq_x[...] = matmul(qkv_w[:, :width], spread).astype(BF16)
        for i in range(2):
            wkv_x[:, i * 2 * LANES:(i + 1) * 2 * LANES] = matmul(
                qkv_w[:, (1 + i) * width:(2 + i) * width], spread).astype(BF16)
        weights[1].wait()
        wo_x[...] = lax.dot_general(
            spread, wo_w[...], (((0,), (0,)), ((), ())), preferred_element_type=F32).astype(BF16)

    def fold_queries():
        scale = 1.4426950408889634 / ((width // H) ** 0.5)
        queries = (matmul(normed[...], wq_x[...]) * scale).astype(BF16)
        lanes = lax.broadcasted_iota(jnp.int32, (tokens, LANES), 1)
        for g in range(2):
            part = queries[:, g * LANES:(g + 1) * LANES]
            for i in range(HEADS):
                one = jnp.where(
                    lanes // 32 == i, part, jnp.where(lanes == SPARE, 1.0, 0.0).astype(BF16))
                for b in range(own):
                    q_ref[b, g, i * BLOCK:(i + 1) * BLOCK] = one[b * BLOCK:(b + 1) * BLOCK]

    def project(values):
        lanes = lax.broadcasted_iota(jnp.int32, (1, 4 * LANES), 1)
        inner = lanes & (LANES - 1)
        ones = jnp.where((lanes >= 2 * LANES) & (inner >= SPARE) & (inner < SPARE + HEADS), 1.0, 0.0)
        return (matmul(values, wkv_x[...]) + ones).astype(BF16)

    def project_far(m, k):
        rows = ROWS[m]
        at, count = ring_places(k)
        plane_copy(m, k, 1, NJ - 1).wait_recv()
        for o in range(0, NJ, 4):
            got = project(far[m][o:o + 4, at:at + count].reshape(4 * count * rows, width))
            kv_far[m][o:o + 4, at:at + count] = got.reshape(4, count, rows, 4 * LANES)

    def project_near(o):
        if o:
            near_copy(o).wait_recv()
        got = project(near[o].reshape(own * BLOCK, width))
        first = 0
        for m, rows in enumerate(ROWS):
            for b in range(own):
                kv_near[m][o, b] = got[b * BLOCK + first:b * BLOCK + first + rows]
            first += rows

    def attend(m, b):
        rows = ROWS[m]
        keys = (NNEAR + NFAR) * rows
        lanes = lax.broadcasted_iota(jnp.int32, (rows, 2 * LANES), 1)
        is_bias = (lanes & (LANES - 1)) == SPARE
        for n in range(NNEAR + NFAR):
            block = kb_ref[b, n]
            owner = block >> 5
            within = block & 31
            bias = jnp.where(within < counts_ref[owner], 0.0, -1e30)
            if n < NNEAR:
                got = kv_near[m][(x - (within >> 3)) & (NX - 1), within & 7]
            else:
                z_rel = ((owner >> 3) - z) & (NZ - 1)
                at = jnp.where(z_rel == 0, 0, jnp.where(
                    z_rel == 8, 15, jnp.where(z_rel < 8, 2 * z_rel - 1, 2 * (NZ - z_rel))))
                got = kv_far[m][(j - (owner & 7)) & (NJ - 1), at]
            part = slice(n * rows, (n + 1) * rows)
            stage[part, :2 * LANES] = jnp.where(is_bias, bias.astype(BF16), got[:, :2 * LANES])
            stage[part, 2 * LANES:] = got[:, 2 * LANES:]
        lane_b = lax.broadcasted_iota(jnp.int32, (BLOCK, LANES), 1)
        lane_t = lax.broadcasted_iota(jnp.int32, (BLOCK, 128), 1)
        for g in range(2):
            s_ref[:, :keys] = lax.dot_general(
                q_ref[b, g], stage[:keys, g * LANES:(g + 1) * LANES], (((1,), (1,)), ((), ())),
                preferred_element_type=F32)
            tops, alphas = [], []
            for i in range(HEADS):
                part = slice(i * BLOCK, (i + 1) * BLOCK)
                scores = s_ref[part, :keys]
                top = jnp.max(scores, axis=-1, keepdims=True)
                if m > 0:
                    before = top_ref[b, g, :, i:i + 1]
                    top = jnp.maximum(top, before)
                    alphas.append(jnp.exp2(before - top))
                tops.append(top)
                p_ref[part, :keys] = jnp.exp2(scores - top).astype(BF16)
            mixed = matmul(p_ref[:, :keys], stage[:keys, (2 + g) * LANES:(3 + g) * LANES])
            total = jnp.zeros((BLOCK, LANES), F32)
            kept = jnp.zeros((BLOCK, LANES), F32)
            for i in range(HEADS):
                mine = (lane_b // 32 == i) | (lane_b == SPARE + i)
                total = jnp.where(mine, mixed[i * BLOCK:(i + 1) * BLOCK], total)
                if m > 0:
                    kept = jnp.where(mine, alphas[i], kept)
            if m > 0:
                total = total + kept * acc_ref[b, g]
            if m < passes - 1:
                acc_ref[b, g] = total
                highest = jnp.zeros((BLOCK, 128), F32)
                for i in range(HEADS):
                    highest = jnp.where(lane_t == i, tops[i], highest)
                top_ref[b, g] = highest
            else:
                denom = jnp.ones((BLOCK, LANES), F32)
                for i in range(HEADS):
                    denom = jnp.where(lane_b // 32 == i, total[:, SPARE + i:SPARE + i + 1], denom)
                result = jnp.where(lane_b < SPARE, total / denom, 0.0)
                att[pl.ds(b * BLOCK, BLOCK), g * LANES:(g + 1) * LANES] = result.astype(BF16)

    def start_ring(m):
        for h in range(PIECES):
            ring(m, 1, h, True).start()
            ring(m, 1, h, False).start()

    for o in range(1, NJ):
        req_copy(o).start()
    start_ring(0)
    for o in range(1, NX):
        near_copy(o).start()
    for o in range(1, NJ):
        req_copy(o).wait_recv()
    copy = pltpu.make_async_copy(req_in, req_s, loc_sem.at[4])
    copy.start()
    copy.wait()

    ticks = [(m, k) for m in range(passes) for k in range(9)]
    work = {}

    def put(tick, task):
        work.setdefault(tick, []).append(task)

    put(0, prepare)
    put(0, fold_queries)
    for o in range(NX):
        put(1 + o, functools.partial(project_near, o))
    for t, (m, k) in enumerate(ticks):
        put(t + 2, functools.partial(project_far, m, k))
    for m in range(passes - 1):
        for b in range(own):
            put(9 * m + 10 + b, functools.partial(attend, m, b))

    for t, (m, k) in enumerate(ticks):
        if k > 0:
            for h in range(PIECES):
                for up in (True, False):
                    if in_ring(k, h, up):
                        ring(m, k, h, up).wait_recv()
                        if in_ring(k + 1, h, up):
                            ring(m, k + 1, h, up).start()
            if k == 7 and m + 1 < passes:
                start_ring(m + 1)
        to_plane(m, k)
        for task in work.pop(t, []):
            task()
    for t in sorted(work):
        for task in work[t]:
            task()

    def last(b, carry):
        attend(passes - 1, b)
        return carry

    lax.fori_loop(0, own, last, 0)

    residual = (tok_ref[...].astype(F32) + matmul(att[...], wo_x[...])).astype(BF16).astype(F32)
    second = rms_norm(residual, gain2_ref[...]).astype(BF16)
    weights[2].wait()
    hidden = jax.nn.gelu(matmul(second, up_w[...])).astype(BF16)
    weights[3].wait()
    out_ref[...] = (residual + matmul(hidden, down_w[...])).astype(BF16)

    for m, k in ticks:
        for h in range(PIECES):
            for up in (True, False):
                if k > 0 and in_ring(k, h, up):
                    ring(m, k, h, up).wait_send()
        plane_copy(m, k, 1, NJ - 1).wait_send()
    for o in range(1, NX):
        near_copy(o).wait_send()
    for o in range(1, NJ):
        req_copy(o).wait_send()


def body(
    tokens, key_blocks, counts, norm_gain, qkv_weight, out_weight, mlp_gain, up_weight, down_weight
):
    count, width = tokens.shape
    own = key_blocks.shape[0]
    passes = len(ROWS)
    vmem = pl.BlockSpec(memory_space=pltpu.VMEM)
    smem = pl.BlockSpec(memory_space=pltpu.SMEM)
    anywhere = pl.BlockSpec(memory_space=pl.ANY)
    dma = pltpu.SemaphoreType.DMA

    def buffers(*shape):
        return [pltpu.VMEM(tuple(rows if n == "rows" else n for n in shape), BF16) for rows in ROWS]

    slots = [pltpu.VMEM((own, rows, width), BF16) for rows in ROWS for _ in range(15)]
    keys = (NNEAR + NFAR) * max(ROWS)
    return pl.pallas_call(
        fused_kernel,
        name="block",
        out_shape=jax.ShapeDtypeStruct(tokens.shape, BF16),
        in_specs=[smem] * 2 + [vmem] * 3 + [anywhere] * 4,
        out_specs=vmem,
        scratch_shapes=buffers(own, "rows", width)
        + slots
        + buffers(NJ, NZ, "rows", width)
        + buffers(NJ, NZ, "rows", width)
        + buffers(NJ, NZ, "rows", 4 * LANES)
        + buffers(NX, own, "rows", 4 * LANES)
        + [
            pltpu.VMEM((NX, own, BLOCK, width), BF16),
            pltpu.VMEM((count, width), BF16),
            pltpu.VMEM(qkv_weight.shape, BF16),
            pltpu.VMEM(out_weight.shape, BF16),
            pltpu.VMEM(up_weight.shape, BF16),
            pltpu.VMEM(down_weight.shape, BF16),
            pltpu.VMEM((width, 2 * LANES), BF16),
            pltpu.VMEM((width, 4 * LANES), BF16),
            pltpu.VMEM((2 * LANES, width), BF16),
            pltpu.VMEM((own, 2, HEADS * BLOCK, LANES), BF16),
            pltpu.VMEM((keys, 4 * LANES), BF16),
            pltpu.VMEM((HEADS * BLOCK, keys), F32),
            pltpu.VMEM((HEADS * BLOCK, keys), BF16),
            pltpu.VMEM((own, 2, BLOCK, LANES), F32),
            pltpu.VMEM((own, 2, BLOCK, 128), F32),
            pltpu.VMEM((count, 2 * LANES), BF16),
            pltpu.VMEM((NJ, 1, 128), jnp.int32),
            pltpu.VMEM((NJ, 1, 128), jnp.int32),
            pltpu.SMEM((NJ, 1, 128), jnp.int32),
            dma((passes, 9, PIECES)), dma((passes, 9, PIECES)), dma((passes, 9, PIECES)), dma((passes, 9, PIECES)),
            dma((passes, 9)), dma((passes, 9)),
            dma((NX,)), dma((NX,)),
            dma((NJ,)), dma((NJ,)),
            dma((5,)),
        ],
        compiler_params=pltpu.CompilerParams(
            collective_id=0, has_side_effects=True, vmem_limit_bytes=62 << 20
        ),
    )(key_blocks, counts, tokens, norm_gain, mlp_gain, qkv_weight, out_weight, up_weight, down_weight)


def solution(mesh):
    return jax.shard_map(
        body,
        mesh=mesh,
        in_specs=(
            P(("gz", "row"), None),
            P(("gz", "row"), None),
            P(),
            P(),
            P(),
            P(),
            P(),
            P(),
            P(),
        ),
        out_specs=P(("gz", "row"), None),
        check_vma=False,
    )
```

```python
import functools

import jax
import jax.numpy as jnp
from jax import lax
from jax.experimental import pallas as pl
from jax.experimental.pallas import tpu as pltpu
from jax.sharding import PartitionSpec as P

H = 12
NNEAR = 4
NFAR = 16
NZ = 16
NJ = 8
NX = 4
BLOCK = 64
HEADS = 6
LANES = 256
SPARE = 192
ROWS = (32, 32)
LAG = 2
PIECES = 2
MESH = pl.DeviceIdType.MESH
F32, BF16 = jnp.float32, jnp.bfloat16


def rms_norm(values, gain):
    mean_sq = jnp.mean(values * values, axis=-1, keepdims=True)
    return values * lax.rsqrt(mean_sq + 1e-05) * gain


def matmul(a, b):
    return jnp.dot(a, b, preferred_element_type=F32)


def ring_places(k):
    return (0, 1) if k == 0 else (15, 1) if k == 8 else (2 * k - 1, 2)


def fused_kernel(
    kb_ref, counts_ref, tok_ref, gain_ref, gain2_ref, qkv_any, wo_any, up_any, down_any, out_ref, *scratch
):
    scratch = list(scratch)
    passes = len(ROWS)

    def take(n):
        got = scratch[:n]
        del scratch[:n]
        return got

    own_rows = take(passes)
    slots = [take(15) for _ in range(passes)]
    send = take(passes)
    far = take(passes)
    kv_far = take(passes)
    kv_near = take(passes)
    near, normed, qkv_w, wo_w, up_w, down_w = take(6)
    wq_x, wkv_x, wo_x, q_ref, acc_ref, top_ref, att = take(7)
    stages, s_refs, p_refs = take(2), take(4), take(4)
    req_out, req_in, req_s = take(3)
    fs_sem, fr_sem, bs_sem, br_sem, ys_sem, yr_sem, xs_sem, xr_sem, qs_sem, qr_sem, loc_sem = take(11)

    tokens, width = tok_ref.shape
    own = tokens // BLOCK
    gz = lax.axis_index("gz")
    x = lax.axis_index("row")
    z = gz // NJ
    j = lax.rem(gz, NJ)
    z_up = lax.rem(z + 1, NZ) * NJ + j
    z_down = lax.rem(z + NZ - 1, NZ) * NJ + j

    def plane(o):
        return z * NJ + lax.rem(j + o, NJ)

    def along(o):
        return lax.rem(x + o, NX)

    barrier = pltpu.get_barrier_semaphore()
    for peer in (z_up, z_down):
        pl.semaphore_signal(barrier, inc=1, device_id=(peer, x), device_id_type=MESH)
    for o in range(1, NJ):
        pl.semaphore_signal(barrier, inc=1, device_id=(plane(o), x), device_id_type=MESH)
    for o in range(1, NX):
        pl.semaphore_signal(barrier, inc=1, device_id=(gz, along(o)), device_id_type=MESH)

    weights = [
        pltpu.make_async_copy(src, dst, loc_sem.at[i])
        for i, (src, dst) in enumerate(
            ((qkv_any, qkv_w), (wo_any, wo_w), (up_any, up_w), (down_any, down_w)))
    ]
    for copy in weights:
        copy.start()

    normed[...] = rms_norm(tok_ref[...].astype(F32), gain_ref[...]).astype(BF16)
    first = 0
    for m, rows in enumerate(ROWS):
        for b in range(own):
            own_rows[m][b] = normed[b * BLOCK + first:b * BLOCK + first + rows]
        first += rows
    pl.semaphore_wait(barrier, 2 + NJ - 1 + NX - 1)

    def make_requests():
        place = lax.broadcasted_iota(jnp.int32, (NJ, 128), 1)
        offset = lax.broadcasted_iota(jnp.int32, (NJ, 128), 0)
        z_off = jnp.where(place == 15, 8, jnp.where((place & 1) == 1, (place + 1) >> 1, NZ - (place >> 1)))
        slab = ((z + z_off) & (NZ - 1)) * NJ + ((j + offset) & (NJ - 1))
        wanted = jnp.zeros((NJ, 128), jnp.int32)
        for b in range(own):
            for n in range(NNEAR, NNEAR + NFAR):
                block = kb_ref[b, n]
                wanted = jnp.where(slab == (block >> 5), block & 7, wanted)
        for r in range(NJ):
            req_out[r] = wanted[r:r + 1]
        req_in[0] = wanted[0:1]

    def req_copy(o):
        return pltpu.make_async_remote_copy(
            src_ref=req_out.at[NJ - o], dst_ref=req_in.at[o],
            send_sem=qs_sem.at[o], recv_sem=qr_sem.at[o],
            device_id=(plane(NJ - o), x), device_id_type=MESH)

    def ring(m, k, h, up):
        src = own_rows[m] if k == 1 else slots[m][(0 if up else 7) + k - 2]
        dst = slots[m][14] if k == 8 else slots[m][(0 if up else 7) + k - 1]
        size = NJ // PIECES
        part = pl.ds(h * size, size)
        return pltpu.make_async_remote_copy(
            src_ref=src.at[part], dst_ref=dst.at[part],
            send_sem=(fs_sem if up else bs_sem).at[m, k, h],
            recv_sem=(fr_sem if up else br_sem).at[m, k, h],
            device_id=(z_up if up else z_down, x), device_id_type=MESH)

    def in_ring(k, h, up):
        return k < 8 or (k == 8 and (h < PIECES // 2) == up)

    def near_copy(o):
        return pltpu.make_async_remote_copy(
            src_ref=near.at[0], dst_ref=near.at[o],
            send_sem=xs_sem.at[o], recv_sem=xr_sem.at[o],
            device_id=(gz, along(o)), device_id_type=MESH)

    def plane_copy(m, k, o, count):
        at = pl.ds(*ring_places(k))
        to = pl.ds(o, count)
        return pltpu.make_async_remote_copy(
            src_ref=send[m].at[to, at], dst_ref=far[m].at[to, at],
            send_sem=ys_sem.at[m, k], recv_sem=yr_sem.at[m, k],
            device_id=(plane(o), x), device_id_type=MESH)

    def to_plane(m, k):
        at, count = ring_places(k)
        if k == 0:
            held = [(0, own_rows[m])]
        elif k == 8:
            held = [(15, slots[m][14])]
        else:
            held = [(at, slots[m][7 + k - 1]), (at + 1, slots[m][k - 1])]

        def one(o, carry):
            for p, ref in held:
                send[m][o, p] = ref[req_s[o, 0, p]]
            plane_copy(m, k, o, 1).start()
            return carry

        lax.fori_loop(1, NJ, one, 0)
        for p, ref in held:
            far[m][0, p] = ref[req_s[0, 0, p]]

    lane = lax.broadcasted_iota(jnp.int32, (1, LANES), 1)

    def prepare():
        row = lax.broadcasted_iota(jnp.int32, (width, 2 * LANES), 0)
        col = lax.broadcasted_iota(jnp.int32, (width, 2 * LANES), 1)
        inner = col & (LANES - 1)
        spread = ((inner < SPARE) & (row == (col >> 8) * SPARE + inner)).astype(F32).astype(BF16)
        weights[0].wait()
        wq_x[...] = matmul(qkv_w[:, :width], spread).astype(BF16)
        for i in range(2):
            wkv_x[:, i * 2 * LANES:(i + 1) * 2 * LANES] = matmul(
                qkv_w[:, (1 + i) * width:(2 + i) * width], spread).astype(BF16)
        weights[1].wait()
        wo_x[...] = lax.dot_general(
            spread, wo_w[...], (((0,), (0,)), ((), ())), preferred_element_type=F32).astype(BF16)

    def fold_queries():
        scale = 1.4426950408889634 / ((width // H) ** 0.5)
        queries = (matmul(normed[...], wq_x[...]) * scale).astype(BF16)
        lanes = lax.broadcasted_iota(jnp.int32, (tokens, LANES), 1)
        for g in range(2):
            part = queries[:, g * LANES:(g + 1) * LANES]
            for i in range(HEADS):
                one = jnp.where(
                    lanes // 32 == i, part, jnp.where(lanes == SPARE, 1.0, 0.0).astype(BF16))
                for b in range(own):
                    q_ref[b, g, i * BLOCK:(i + 1) * BLOCK] = one[b * BLOCK:(b + 1) * BLOCK]

    def project(values):
        lanes = lax.broadcasted_iota(jnp.int32, (1, 4 * LANES), 1)
        inner = lanes & (LANES - 1)
        ones = jnp.where((lanes >= 2 * LANES) & (inner >= SPARE) & (inner < SPARE + HEADS), 1.0, 0.0)
        return (matmul(values, wkv_x[...]) + ones).astype(BF16)

    def project_far(m, k):
        rows = ROWS[m]
        at, count = ring_places(k)
        plane_copy(m, k, 1, NJ - 1).wait_recv()
        for o in range(0, NJ, 4):
            got = project(far[m][o:o + 4, at:at + count].reshape(4 * count * rows, width))
            kv_far[m][o:o + 4, at:at + count] = got.reshape(4, count, rows, 4 * LANES)

    def project_near(o):
        if o:
            near_copy(o).wait_recv()
        got = project(near[o].reshape(own * BLOCK, width))
        first = 0
        for m, rows in enumerate(ROWS):
            for b in range(own):
                kv_near[m][o, b] = got[b * BLOCK + first:b * BLOCK + first + rows]
            first += rows

    lane_b = lax.broadcasted_iota(jnp.int32, (1, LANES), 1)
    lane_t = lax.broadcasted_iota(jnp.int32, (1, 128), 1)
    head_lanes = [(lane_b >> 5) == i for i in range(HEADS)]
    mine = [head_lanes[i] | (lane_b == SPARE + i) for i in range(HEADS)]

    def fill(m, b, stage):
        rows = ROWS[m]
        lanes = lax.broadcasted_iota(jnp.int32, (rows, 2 * LANES), 1)
        is_bias = (lanes & (LANES - 1)) == SPARE
        for n in range(NNEAR + NFAR):
            block = kb_ref[b, n]
            owner = block >> 5
            within = block & 31
            bias = jnp.where(within < counts_ref[owner], 0.0, -1e30)
            if n < NNEAR:
                got = kv_near[m][(x - (within >> 3)) & (NX - 1), within & 7]
            else:
                z_rel = ((owner >> 3) - z) & (NZ - 1)
                at = jnp.where(z_rel == 0, 0, jnp.where(
                    z_rel == 8, 15, jnp.where(z_rel < 8, 2 * z_rel - 1, 2 * (NZ - z_rel))))
                got = kv_far[m][(j - (owner & 7)) & (NJ - 1), at]
            part = slice(n * rows, (n + 1) * rows)
            stage[part, :2 * LANES] = jnp.where(is_bias, bias.astype(BF16), got[:, :2 * LANES])
            stage[part, 2 * LANES:] = got[:, 2 * LANES:]

    def softmax(m, s_ref, p_ref):
        keys = (NNEAR + NFAR) * ROWS[m]
        tops = []
        for i in range(HEADS):
            part = slice(i * BLOCK, (i + 1) * BLOCK)
            scores = s_ref[part, :keys]
            top = jnp.max(scores, axis=-1, keepdims=True)
            tops.append(top)
            p_ref[part, :keys] = jnp.exp2(scores - top).astype(BF16)
        return tops

    def keep(m, b, g, mixed, tops):
        total = jnp.zeros((BLOCK, LANES), F32)
        highest = jnp.zeros((BLOCK, 128), F32)
        for i in range(HEADS):
            total = jnp.where(mine[i], mixed[i * BLOCK:(i + 1) * BLOCK], total)
            highest = jnp.where(lane_t == i, tops[i], highest)
        rows = pl.ds(b * BLOCK, BLOCK)
        acc_ref[m, g, rows] = total
        top_ref[m, g, rows] = highest

    def select(values, chosen):
        high = values.astype(BF16)
        low = (values - high.astype(F32)).astype(BF16)
        return matmul(high, chosen) + matmul(low, chosen)

    def join():
        row = lax.broadcasted_iota(jnp.int32, (128, LANES), 0)
        col = lax.broadcasted_iota(jnp.int32, (128, LANES), 1)
        spread = ((row < HEADS) & ((row == (col >> 5)) | (col == SPARE + row))).astype(F32).astype(BF16)
        row = lax.broadcasted_iota(jnp.int32, (LANES, LANES), 0)
        col = lax.broadcasted_iota(jnp.int32, (LANES, LANES), 1)
        source = jnp.where(col < SPARE, SPARE + (col >> 5), SPARE)
        totals = (row == source).astype(F32).astype(BF16)
        for g in range(2):
            tops = [top_ref[m, g] for m in range(passes)]
            highest = functools.reduce(jnp.maximum, tops)
            total = sum(
                select(jnp.exp2(tops[m] - highest), spread) * acc_ref[m, g] for m in range(passes))
            result = jnp.where(lane_b < SPARE, total / select(total, totals), 0.0)
            att[:, g * LANES:(g + 1) * LANES] = result.astype(BF16)

    def attend(m, first):
        keys = (NNEAR + NFAR) * ROWS[m]
        chains = [(c, first + c // 2, c % 2) for c in range(4)]
        for c in range(2):
            fill(m, first + c, stages[c])
        for c, b, g in chains:
            s_refs[c][:, :keys] = lax.dot_general(
                q_ref[b, g], stages[c // 2][:keys, g * LANES:(g + 1) * LANES], (((1,), (1,)), ((), ())),
                preferred_element_type=F32)
        found = [softmax(m, s_refs[c], p_refs[c]) for c, b, g in chains]
        for c, b, g in chains:
            mixed = matmul(p_refs[c][:, :keys], stages[c // 2][:keys, (2 + g) * LANES:(3 + g) * LANES])
            keep(m, b, g, mixed, found[c])

    def start_ring(m):
        for h in range(PIECES):
            ring(m, 1, h, True).start()
            ring(m, 1, h, False).start()

    start_ring(0)
    make_requests()
    for o in range(1, NJ):
        req_copy(o).start()
    for b in range(own):
        near[0, b] = normed[b * BLOCK:(b + 1) * BLOCK]
    for o in range(1, NX):
        near_copy(o).start()
    for o in range(1, NJ):
        req_copy(o).wait_recv()
    copy = pltpu.make_async_copy(req_in, req_s, loc_sem.at[4])
    copy.start()
    copy.wait()

    ticks = 9 + LAG * (passes - 1)
    work = {}

    def put(tick, task):
        work.setdefault(tick, []).append(task)

    put(0, prepare)
    put(0, fold_queries)
    for o in range(NX):
        put(1 + o, functools.partial(project_near, o))
    for t in range(ticks):
        for m in range(passes):
            if 0 <= t - m * LAG <= 8:
                put(t + 1, functools.partial(project_far, m, t - m * LAG))
    for m in range(passes - 1):
        for i in range(own // 2):
            put(min(9 + m * LAG + i, ticks - 1), functools.partial(attend, m, 2 * i))

    for t in range(ticks):
        active = [(m, t - m * LAG) for m in range(passes) if 0 <= t - m * LAG <= 8]
        for m, k in active:
            if k == 0:
                if m:
                    start_ring(m)
                continue
            for h in range(PIECES):
                for up in (True, False):
                    if in_ring(k, h, up):
                        ring(m, k, h, up).wait_recv()
                        if in_ring(k + 1, h, up):
                            ring(m, k + 1, h, up).start()
        for m, k in active:
            to_plane(m, k)
        for task in work.pop(t, []):
            task()
    for t in sorted(work):
        for task in work[t]:
            task()

    def last(i, carry):
        attend(passes - 1, 2 * i)
        return carry

    lax.fori_loop(0, own // 2, last, 0)
    join()

    residual = (tok_ref[...].astype(F32) + matmul(att[...], wo_x[...])).astype(BF16).astype(F32)
    second = rms_norm(residual, gain2_ref[...]).astype(BF16)
    weights[2].wait()
    hidden = jax.nn.gelu(matmul(second, up_w[...])).astype(BF16)
    weights[3].wait()
    out_ref[...] = (residual + matmul(hidden, down_w[...])).astype(BF16)

    for m, k in [(m, k) for m in range(passes) for k in range(9)]:
        for h in range(PIECES):
            for up in (True, False):
                if k > 0 and in_ring(k, h, up):
                    ring(m, k, h, up).wait_send()
        plane_copy(m, k, 1, NJ - 1).wait_send()
    for o in range(1, NX):
        near_copy(o).wait_send()
    for o in range(1, NJ):
        req_copy(o).wait_send()


def body(
    tokens, key_blocks, counts, norm_gain, qkv_weight, out_weight, mlp_gain, up_weight, down_weight
):
    count, width = tokens.shape
    own = key_blocks.shape[0]
    passes = len(ROWS)
    vmem = pl.BlockSpec(memory_space=pltpu.VMEM)
    smem = pl.BlockSpec(memory_space=pltpu.SMEM)
    anywhere = pl.BlockSpec(memory_space=pl.ANY)
    dma = pltpu.SemaphoreType.DMA

    def buffers(*shape):
        return [pltpu.VMEM(tuple(rows if n == "rows" else n for n in shape), BF16) for rows in ROWS]

    slots = [pltpu.VMEM((own, rows, width), BF16) for rows in ROWS for _ in range(15)]
    keys = (NNEAR + NFAR) * max(ROWS)
    return pl.pallas_call(
        fused_kernel,
        name="block",
        out_shape=jax.ShapeDtypeStruct(tokens.shape, BF16),
        in_specs=[smem] * 2 + [vmem] * 3 + [anywhere] * 4,
        out_specs=vmem,
        scratch_shapes=buffers(own, "rows", width)
        + slots
        + buffers(NJ, NZ, "rows", width)
        + buffers(NJ, NZ, "rows", width)
        + buffers(NJ, NZ, "rows", 4 * LANES)
        + buffers(NX, own, "rows", 4 * LANES)
        + [
            pltpu.VMEM((NX, own, BLOCK, width), BF16),
            pltpu.VMEM((count, width), BF16),
            pltpu.VMEM(qkv_weight.shape, BF16),
            pltpu.VMEM(out_weight.shape, BF16),
            pltpu.VMEM(up_weight.shape, BF16),
            pltpu.VMEM(down_weight.shape, BF16),
            pltpu.VMEM((width, 2 * LANES), BF16),
            pltpu.VMEM((width, 4 * LANES), BF16),
            pltpu.VMEM((2 * LANES, width), BF16),
            pltpu.VMEM((own, 2, HEADS * BLOCK, LANES), BF16),
            pltpu.VMEM((passes, 2, count, LANES), F32),
            pltpu.VMEM((passes, 2, count, 128), F32),
            pltpu.VMEM((count, 2 * LANES), BF16),
        ]
        + [pltpu.VMEM((keys, 4 * LANES), BF16)] * 2
        + [pltpu.VMEM((HEADS * BLOCK, keys), F32)] * 4
        + [pltpu.VMEM((HEADS * BLOCK, keys), BF16)] * 4
        + [
            pltpu.VMEM((NJ, 1, 128), jnp.int32),
            pltpu.VMEM((NJ, 1, 128), jnp.int32),
            pltpu.SMEM((NJ, 1, 128), jnp.int32),
            dma((passes, 9, PIECES)), dma((passes, 9, PIECES)), dma((passes, 9, PIECES)), dma((passes, 9, PIECES)),
            dma((passes, 9)), dma((passes, 9)),
            dma((NX,)), dma((NX,)),
            dma((NJ,)), dma((NJ,)),
            dma((5,)),
        ],
        compiler_params=pltpu.CompilerParams(
            collective_id=0, has_side_effects=True, vmem_limit_bytes=62 << 20
        ),
    )(key_blocks, counts, tokens, norm_gain, mlp_gain, qkv_weight, out_weight, up_weight, down_weight)


def solution(mesh):
    return jax.shard_map(
        body,
        mesh=mesh,
        in_specs=(
            P(("gz", "row"), None),
            P(("gz", "row"), None),
            P(),
            P(),
            P(),
            P(),
            P(),
            P(),
            P(),
        ),
        out_specs=P(("gz", "row"), None),
        check_vma=False,
    )
```

```python
import functools

import jax
import jax.numpy as jnp
from jax import lax
from jax.experimental import pallas as pl
from jax.experimental.pallas import tpu as pltpu
from jax.sharding import PartitionSpec as P

H = 12
NNEAR = 4
NFAR = 16
NZ = 16
NJ = 8
NX = 4
BLOCK = 64
HEADS = 6
LANES = 256
SPARE = 192
ROWS = (32, 32)
LAG = 2
PIECES = 1
MESH = pl.DeviceIdType.MESH
F32, BF16 = jnp.float32, jnp.bfloat16


def rms_norm(values, gain):
    mean_sq = jnp.mean(values * values, axis=-1, keepdims=True)
    return values * lax.rsqrt(mean_sq + 1e-05) * gain


def matmul(a, b):
    return jnp.dot(a, b, preferred_element_type=F32)


def ring_places(k):
    return (0, 1) if k == 0 else (15, 1) if k == 8 else (2 * k - 1, 2)


def fused_kernel(
    kb_ref, counts_ref, tok_ref, gain_ref, gain2_ref, qkv_any, wo_any, up_any, down_any, out_ref, *scratch
):
    scratch = list(scratch)
    passes = len(ROWS)

    def take(n):
        got = scratch[:n]
        del scratch[:n]
        return got

    own_rows = take(passes)
    slots = [take(15) for _ in range(passes)]
    send = take(passes)
    far = take(passes)
    kv_far = take(passes)
    kv_near = take(passes)
    near, normed, qkv_w, wo_w, up_w, down_w = take(6)
    wq_x, wkv_x, wo_x, q_ref, acc_ref, top_ref, att = take(7)
    stages, s_refs, p_refs = take(2), take(4), take(4)
    req_out, req_in, req_s = take(3)
    fs_sem, fr_sem, bs_sem, br_sem, ys_sem, yr_sem, xs_sem, xr_sem, qs_sem, qr_sem, loc_sem = take(11)

    tokens, width = tok_ref.shape
    own = tokens // BLOCK
    gz = lax.axis_index("gz")
    x = lax.axis_index("row")
    z = gz // NJ
    j = lax.rem(gz, NJ)
    z_up = lax.rem(z + 1, NZ) * NJ + j
    z_down = lax.rem(z + NZ - 1, NZ) * NJ + j

    def plane(o):
        return z * NJ + lax.rem(j + o, NJ)

    def along(o):
        return lax.rem(x + o, NX)

    barrier = pltpu.get_barrier_semaphore()
    for peer in (z_up, z_down):
        pl.semaphore_signal(barrier, inc=1, device_id=(peer, x), device_id_type=MESH)
    for o in range(1, NJ):
        pl.semaphore_signal(barrier, inc=1, device_id=(plane(o), x), device_id_type=MESH)
    for o in range(1, NX):
        pl.semaphore_signal(barrier, inc=1, device_id=(gz, along(o)), device_id_type=MESH)

    weights = [
        pltpu.make_async_copy(src, dst, loc_sem.at[i])
        for i, (src, dst) in enumerate(
            ((qkv_any, qkv_w), (wo_any, wo_w), (up_any, up_w), (down_any, down_w)))
    ]
    for copy in weights:
        copy.start()

    normed[...] = rms_norm(tok_ref[...].astype(F32), gain_ref[...]).astype(BF16)
    first = 0
    for m, rows in enumerate(ROWS):
        for b in range(own):
            own_rows[m][b] = normed[b * BLOCK + first:b * BLOCK + first + rows]
        first += rows
    pl.semaphore_wait(barrier, 2 + NJ - 1 + NX - 1)

    def make_requests():
        place = lax.broadcasted_iota(jnp.int32, (NJ, 128), 1)
        offset = lax.broadcasted_iota(jnp.int32, (NJ, 128), 0)
        z_off = jnp.where(place == 15, 8, jnp.where((place & 1) == 1, (place + 1) >> 1, NZ - (place >> 1)))
        slab = ((z + z_off) & (NZ - 1)) * NJ + ((j + offset) & (NJ - 1))
        wanted = jnp.zeros((NJ, 128), jnp.int32)
        for b in range(own):
            for n in range(NNEAR, NNEAR + NFAR):
                block = kb_ref[b, n]
                wanted = jnp.where(slab == (block >> 5), block & 7, wanted)
        for r in range(NJ):
            req_out[r] = wanted[r:r + 1]
        req_in[0] = wanted[0:1]

    def req_copy(o):
        return pltpu.make_async_remote_copy(
            src_ref=req_out.at[NJ - o], dst_ref=req_in.at[o],
            send_sem=qs_sem.at[o], recv_sem=qr_sem.at[o],
            device_id=(plane(NJ - o), x), device_id_type=MESH)

    def ring(m, k, h, up):
        src = own_rows[m] if k == 1 else slots[m][(0 if up else 7) + k - 2]
        dst = slots[m][14] if k == 8 else slots[m][(0 if up else 7) + k - 1]
        size = NJ // PIECES
        part = pl.ds(h * size, size)
        return pltpu.make_async_remote_copy(
            src_ref=src.at[part], dst_ref=dst.at[part],
            send_sem=(fs_sem if up else bs_sem).at[m, k, h],
            recv_sem=(fr_sem if up else br_sem).at[m, k, h],
            device_id=(z_up if up else z_down, x), device_id_type=MESH)

    def in_ring(m, k, h, up):
        return k < 8 or (k == 8 and (m % 2 == 1) == up)

    def near_copy(o):
        return pltpu.make_async_remote_copy(
            src_ref=near.at[0], dst_ref=near.at[o],
            send_sem=xs_sem.at[o], recv_sem=xr_sem.at[o],
            device_id=(gz, along(o)), device_id_type=MESH)

    def plane_copy(m, k, o, count):
        at = pl.ds(*ring_places(k))
        to = pl.ds(o, count)
        return pltpu.make_async_remote_copy(
            src_ref=send[m].at[to, at], dst_ref=far[m].at[to, at],
            send_sem=ys_sem.at[m, k], recv_sem=yr_sem.at[m, k],
            device_id=(plane(o), x), device_id_type=MESH)

    def to_plane(m, k):
        at, count = ring_places(k)
        if k == 0:
            held = [(0, own_rows[m])]
        elif k == 8:
            held = [(15, slots[m][14])]
        else:
            held = [(at, slots[m][7 + k - 1]), (at + 1, slots[m][k - 1])]

        def one(o, carry):
            for p, ref in held:
                send[m][o, p] = ref[req_s[o, 0, p]]
            plane_copy(m, k, o, 1).start()
            return carry

        lax.fori_loop(1, NJ, one, 0)
        for p, ref in held:
            far[m][0, p] = ref[req_s[0, 0, p]]

    lane = lax.broadcasted_iota(jnp.int32, (1, LANES), 1)

    def prepare():
        row = lax.broadcasted_iota(jnp.int32, (width, 2 * LANES), 0)
        col = lax.broadcasted_iota(jnp.int32, (width, 2 * LANES), 1)
        inner = col & (LANES - 1)
        spread = ((inner < SPARE) & (row == (col >> 8) * SPARE + inner)).astype(F32).astype(BF16)
        weights[0].wait()
        wq_x[...] = matmul(qkv_w[:, :width], spread).astype(BF16)
        for i in range(2):
            wkv_x[:, i * 2 * LANES:(i + 1) * 2 * LANES] = matmul(
                qkv_w[:, (1 + i) * width:(2 + i) * width], spread).astype(BF16)
        weights[1].wait()
        wo_x[...] = lax.dot_general(
            spread, wo_w[...], (((0,), (0,)), ((), ())), preferred_element_type=F32).astype(BF16)

    def fold_queries():
        scale = 1.4426950408889634 / ((width // H) ** 0.5)
        queries = (matmul(normed[...], wq_x[...]) * scale).astype(BF16)
        lanes = lax.broadcasted_iota(jnp.int32, (tokens, LANES), 1)
        for g in range(2):
            part = queries[:, g * LANES:(g + 1) * LANES]
            for i in range(HEADS):
                one = jnp.where(
                    lanes // 32 == i, part, jnp.where(lanes == SPARE, 1.0, 0.0).astype(BF16))
                for b in range(own):
                    q_ref[b, g, i * BLOCK:(i + 1) * BLOCK] = one[b * BLOCK:(b + 1) * BLOCK]

    def project(values):
        lanes = lax.broadcasted_iota(jnp.int32, (1, 4 * LANES), 1)
        inner = lanes & (LANES - 1)
        ones = jnp.where((lanes >= 2 * LANES) & (inner >= SPARE) & (inner < SPARE + HEADS), 1.0, 0.0)
        return (matmul(values, wkv_x[...]) + ones).astype(BF16)

    def project_far(m, k):
        rows = ROWS[m]
        at, count = ring_places(k)
        plane_copy(m, k, 1, NJ - 1).wait_recv()
        for o in range(0, NJ, 4):
            got = project(far[m][o:o + 4, at:at + count].reshape(4 * count * rows, width))
            kv_far[m][o:o + 4, at:at + count] = got.reshape(4, count, rows, 4 * LANES)

    def project_near(o):
        if o:
            near_copy(o).wait_recv()
        got = project(near[o].reshape(own * BLOCK, width))
        first = 0
        for m, rows in enumerate(ROWS):
            for b in range(own):
                kv_near[m][o, b] = got[b * BLOCK + first:b * BLOCK + first + rows]
            first += rows

    lane_b = lax.broadcasted_iota(jnp.int32, (1, LANES), 1)
    lane_t = lax.broadcasted_iota(jnp.int32, (1, 128), 1)
    head_lanes = [(lane_b >> 5) == i for i in range(HEADS)]
    mine = [head_lanes[i] | (lane_b == SPARE + i) for i in range(HEADS)]

    def fill(m, b, stage):
        rows = ROWS[m]
        lanes = lax.broadcasted_iota(jnp.int32, (rows, 2 * LANES), 1)
        is_bias = (lanes & (LANES - 1)) == SPARE
        for n in range(NNEAR + NFAR):
            block = kb_ref[b, n]
            owner = block >> 5
            within = block & 31
            bias = jnp.where(within < counts_ref[owner], 0.0, -1e30)
            if n < NNEAR:
                got = kv_near[m][(x - (within >> 3)) & (NX - 1), within & 7]
            else:
                z_rel = ((owner >> 3) - z) & (NZ - 1)
                at = jnp.where(z_rel == 0, 0, jnp.where(
                    z_rel == 8, 15, jnp.where(z_rel < 8, 2 * z_rel - 1, 2 * (NZ - z_rel))))
                got = kv_far[m][(j - (owner & 7)) & (NJ - 1), at]
            part = slice(n * rows, (n + 1) * rows)
            stage[part, :2 * LANES] = jnp.where(is_bias, bias.astype(BF16), got[:, :2 * LANES])
            stage[part, 2 * LANES:] = got[:, 2 * LANES:]

    def softmax(m, s_ref, p_ref):
        keys = (NNEAR + NFAR) * ROWS[m]
        tops = []
        for i in range(HEADS):
            part = slice(i * BLOCK, (i + 1) * BLOCK)
            scores = s_ref[part, :keys]
            top = jnp.max(scores, axis=-1, keepdims=True)
            tops.append(top)
            p_ref[part, :keys] = jnp.exp2(scores - top).astype(BF16)
        return tops

    def keep(m, b, g, mixed, tops):
        total = jnp.zeros((BLOCK, LANES), F32)
        highest = jnp.zeros((BLOCK, 128), F32)
        for i in range(HEADS):
            total = jnp.where(mine[i], mixed[i * BLOCK:(i + 1) * BLOCK], total)
            highest = jnp.where(lane_t == i, tops[i], highest)
        rows = pl.ds(b * BLOCK, BLOCK)
        acc_ref[m, g, rows] = total
        top_ref[m, g, rows] = highest

    def select(values, chosen):
        high = values.astype(BF16)
        low = (values - high.astype(F32)).astype(BF16)
        return matmul(high, chosen) + matmul(low, chosen)

    def join():
        row = lax.broadcasted_iota(jnp.int32, (128, LANES), 0)
        col = lax.broadcasted_iota(jnp.int32, (128, LANES), 1)
        spread = ((row < HEADS) & ((row == (col >> 5)) | (col == SPARE + row))).astype(F32).astype(BF16)
        row = lax.broadcasted_iota(jnp.int32, (LANES, LANES), 0)
        col = lax.broadcasted_iota(jnp.int32, (LANES, LANES), 1)
        source = jnp.where(col < SPARE, SPARE + (col >> 5), SPARE)
        totals = (row == source).astype(F32).astype(BF16)
        for g in range(2):
            tops = [top_ref[m, g] for m in range(passes)]
            highest = functools.reduce(jnp.maximum, tops)
            total = sum(
                select(jnp.exp2(tops[m] - highest), spread) * acc_ref[m, g] for m in range(passes))
            result = jnp.where(lane_b < SPARE, total / select(total, totals), 0.0)
            att[:, g * LANES:(g + 1) * LANES] = result.astype(BF16)

    def attend(m, first):
        keys = (NNEAR + NFAR) * ROWS[m]
        chains = [(c, first + c // 2, c % 2) for c in range(4)]
        for c in range(2):
            fill(m, first + c, stages[c])
        for c, b, g in chains:
            s_refs[c][:, :keys] = lax.dot_general(
                q_ref[b, g], stages[c // 2][:keys, g * LANES:(g + 1) * LANES], (((1,), (1,)), ((), ())),
                preferred_element_type=F32)
        found = [softmax(m, s_refs[c], p_refs[c]) for c, b, g in chains]
        for c, b, g in chains:
            mixed = matmul(p_refs[c][:, :keys], stages[c // 2][:keys, (2 + g) * LANES:(3 + g) * LANES])
            keep(m, b, g, mixed, found[c])

    def start_ring(m):
        for h in range(PIECES):
            ring(m, 1, h, True).start()
            ring(m, 1, h, False).start()

    start_ring(0)
    make_requests()
    for o in range(1, NJ):
        req_copy(o).start()
    for b in range(own):
        near[0, b] = normed[b * BLOCK:(b + 1) * BLOCK]
    for o in range(1, NX):
        near_copy(o).start()
    for o in range(1, NJ):
        req_copy(o).wait_recv()
    copy = pltpu.make_async_copy(req_in, req_s, loc_sem.at[4])
    copy.start()
    copy.wait()

    ticks = 9 + LAG * (passes - 1)
    work = {}

    def put(tick, task):
        work.setdefault(tick, []).append(task)

    put(0, prepare)
    put(0, fold_queries)
    for o in range(NX):
        put(1 + o, functools.partial(project_near, o))
    for t in range(ticks):
        for m in range(passes):
            if 0 <= t - m * LAG <= 8:
                put(t + 1, functools.partial(project_far, m, t - m * LAG))
    for m in range(passes - 1):
        for i in range(own // 2):
            put(min(9 + m * LAG + i, ticks - 1), functools.partial(attend, m, 2 * i))

    for t in range(ticks):
        active = [(m, t - m * LAG) for m in range(passes) if 0 <= t - m * LAG <= 8]
        for m, k in active:
            if k == 0:
                if m:
                    start_ring(m)
                continue
            for h in range(PIECES):
                for up in (True, False):
                    if in_ring(m, k, h, up):
                        ring(m, k, h, up).wait_recv()
                        if in_ring(m, k + 1, h, up):
                            ring(m, k + 1, h, up).start()
        for m, k in active:
            to_plane(m, k)
        for task in work.pop(t, []):
            task()
    for t in sorted(work):
        for task in work[t]:
            task()

    def last(i, carry):
        attend(passes - 1, 2 * i)
        return carry

    lax.fori_loop(0, own // 2, last, 0)
    join()

    residual = (tok_ref[...].astype(F32) + matmul(att[...], wo_x[...])).astype(BF16).astype(F32)
    second = rms_norm(residual, gain2_ref[...]).astype(BF16)
    weights[2].wait()
    weights[3].wait()
    result = residual
    for c in range(0, up_w.shape[1], 512):
        hidden = jax.nn.gelu(matmul(second, up_w[:, c:c + 512])).astype(BF16)
        result = result + matmul(hidden, down_w[c:c + 512])
    out_ref[...] = result.astype(BF16)

    for m, k in [(m, k) for m in range(passes) for k in range(9)]:
        for h in range(PIECES):
            for up in (True, False):
                if k > 0 and in_ring(m, k, h, up):
                    ring(m, k, h, up).wait_send()
        plane_copy(m, k, 1, NJ - 1).wait_send()
    for o in range(1, NX):
        near_copy(o).wait_send()
    for o in range(1, NJ):
        req_copy(o).wait_send()


def body(
    tokens, key_blocks, counts, norm_gain, qkv_weight, out_weight, mlp_gain, up_weight, down_weight
):
    count, width = tokens.shape
    own = key_blocks.shape[0]
    passes = len(ROWS)
    vmem = pl.BlockSpec(memory_space=pltpu.VMEM)
    smem = pl.BlockSpec(memory_space=pltpu.SMEM)
    anywhere = pl.BlockSpec(memory_space=pl.ANY)
    dma = pltpu.SemaphoreType.DMA

    def buffers(*shape):
        return [pltpu.VMEM(tuple(rows if n == "rows" else n for n in shape), BF16) for rows in ROWS]

    slots = [pltpu.VMEM((own, rows, width), BF16) for rows in ROWS for _ in range(15)]
    keys = (NNEAR + NFAR) * max(ROWS)
    return pl.pallas_call(
        fused_kernel,
        name="block",
        out_shape=jax.ShapeDtypeStruct(tokens.shape, BF16),
        in_specs=[smem] * 2 + [vmem] * 3 + [anywhere] * 4,
        out_specs=vmem,
        scratch_shapes=buffers(own, "rows", width)
        + slots
        + buffers(NJ, NZ, "rows", width)
        + buffers(NJ, NZ, "rows", width)
        + buffers(NJ, NZ, "rows", 4 * LANES)
        + buffers(NX, own, "rows", 4 * LANES)
        + [
            pltpu.VMEM((NX, own, BLOCK, width), BF16),
            pltpu.VMEM((count, width), BF16),
            pltpu.VMEM(qkv_weight.shape, BF16),
            pltpu.VMEM(out_weight.shape, BF16),
            pltpu.VMEM(up_weight.shape, BF16),
            pltpu.VMEM(down_weight.shape, BF16),
            pltpu.VMEM((width, 2 * LANES), BF16),
            pltpu.VMEM((width, 4 * LANES), BF16),
            pltpu.VMEM((2 * LANES, width), BF16),
            pltpu.VMEM((own, 2, HEADS * BLOCK, LANES), BF16),
            pltpu.VMEM((passes, 2, count, LANES), F32),
            pltpu.VMEM((passes, 2, count, 128), F32),
            pltpu.VMEM((count, 2 * LANES), BF16),
        ]
        + [pltpu.VMEM((keys, 4 * LANES), BF16)] * 2
        + [pltpu.VMEM((HEADS * BLOCK, keys), F32)] * 4
        + [pltpu.VMEM((HEADS * BLOCK, keys), BF16)] * 4
        + [
            pltpu.VMEM((NJ, 1, 128), jnp.int32),
            pltpu.VMEM((NJ, 1, 128), jnp.int32),
            pltpu.SMEM((NJ, 1, 128), jnp.int32),
            dma((passes, 9, PIECES)), dma((passes, 9, PIECES)), dma((passes, 9, PIECES)), dma((passes, 9, PIECES)),
            dma((passes, 9)), dma((passes, 9)),
            dma((NX,)), dma((NX,)),
            dma((NJ,)), dma((NJ,)),
            dma((5,)),
        ],
        compiler_params=pltpu.CompilerParams(
            collective_id=0, has_side_effects=True, vmem_limit_bytes=62 << 20
        ),
    )(key_blocks, counts, tokens, norm_gain, mlp_gain, qkv_weight, out_weight, up_weight, down_weight)


def solution(mesh):
    return jax.shard_map(
        body,
        mesh=mesh,
        in_specs=(
            P(("gz", "row"), None),
            P(("gz", "row"), None),
            P(),
            P(),
            P(),
            P(),
            P(),
            P(),
            P(),
        ),
        out_specs=P(("gz", "row"), None),
        check_vma=False,
    )
```
